256 devices in a mesh: pipe: 4 (over y_hi, core), ctx: 8 (over y_lo, x), tp: 8 (over z).
Axes of the slice: x: 4, y: 4 (y_hi: 2, y_lo: 2; y = y_hi * 2 + y_lo), z: 8, core: 2. Of those that a mesh axis runs over, the one named last changes fastest.
Arguments:
- section_input: bfloat16 [4, 1024, 8192], P('pipe', 'tp', 'ctx'), may hold values from -42 to 42, as said below
- norm_gain: bfloat16 [4, 8192], P('pipe', 'ctx'), may hold values from 0.099609375 to 1.8984375
- in_weight: bfloat16 [4, 8192, 3, 8192], P('pipe', 'ctx', None, 'tp'), may hold values from -0.0625 to 0.0625
- qkv_filters: bfloat16 [4, 3, 128, 8192], P('pipe', None, None, 'tp'), may hold values from -0.5 to 0.5
- mix_filter: bfloat16 [4, 128, 8192], P('pipe', None, 'tp'), may hold values from -0.5 to 0.5
- out_weight: bfloat16 [4, 8192, 8192], P('pipe', 'tp', 'ctx'), may hold values from -0.0625 to 0.0625
Outputs:
- handed: bfloat16 [4, 1024, 8192], P('pipe', 'tp', 'ctx')
The draws below stay inside these ranges and needn't reach their ends.
Inputs may be any that keep to these rules, and one draw needn't show every extreme that they name: `section_input`: Real-valued activations with position and feature scales of order one.
All inputs are finite; a program needn't handle non-finite values.
Results may differ from the reference program's by a relative error of at most 0.029.
Values may be sent and summed in bfloat16 or wider, within the bound.
No kernel may reach another device: no remote copies, remote signals or barrier semaphores. Data moves between devices by JAX's collectives and lax.ppermute only.
A program may use at most 128 MiB of HBM per device.

```python
import math
import jax
import jax.numpy as jnp
from jax import lax

D = 8192
TAPS = 128
SEGMENT = 1024
SECTIONS = 4
N_CTX = 8


def draw_section_input(key, part):
    key_base, key_rows, key_cols = jax.random.split(key, 3)
    row_scale = jnp.exp(jax.random.uniform(key_rows, (SECTIONS, SEGMENT, 1), jnp.float32, math.log(0.3), math.log(3.0)))
    col_scale = jnp.exp(jax.random.uniform(key_cols, (1, 1, D), jnp.float32, math.log(0.5), math.log(2.0)))
    ramp = jnp.exp(math.log(3.0) * (jnp.arange(D, dtype=jnp.float32) / D - 0.5))
    base_values = jnp.clip(jax.random.normal(key_base, (SECTIONS, SEGMENT, D), jnp.float32), -4.0, 4.0)
    return (base_values * row_scale * col_scale * ramp[None, None, :]).astype(jnp.bfloat16)


def block_levels(rng, dims, cuts, low, top_value):
    level = 1.0
    for axis_at, shards_of in cuts:
        heights = jax.random.uniform(jax.random.fold_in(jax.random.fold_in(rng, 6), axis_at), (shards_of,), jnp.float32, low / len(cuts), top_value / len(cuts))
        level = level * jnp.repeat(jnp.exp(heights), dims[axis_at] // shards_of).reshape((-1,) + (1,) * (len(dims) - 1 - axis_at))
    return level


def bell_draw(stream_key, dims, width, bound, pieces=(), kind=jnp.bfloat16):
    array = jax.random.normal(stream_key, dims, jnp.float32) * width
    if len(pieces) > 0:
        array = block_levels(stream_key, dims, pieces, -0.22, 0.18) * array
    return jnp.clip(array, min=-bound, max=bound).astype(kind)


def setup_inputs(seed: int = 0) -> dict:
    keys = jax.random.split(jax.random.key(seed), 7)
    section_input = draw_section_input(jax.random.fold_in(keys[6], 71), 0)
    norm_gain = jnp.clip(1.0 + 0.18 * jax.random.normal(keys[1], (SECTIONS, D), jnp.float32), 0.099609375, 1.8984375).astype(jnp.bfloat16)
    in_weight = bell_draw(keys[2], (SECTIONS, D, 3, D), D ** -0.5, 0.0625, ((0, 4), (1, 8), (3, 8)))
    qkv_filters = bell_draw(keys[3], (SECTIONS, 3, TAPS, D), TAPS ** -0.5, 0.5, ((0, 4), (3, 8)))
    mix_filter = bell_draw(keys[4], (SECTIONS, TAPS, D), TAPS ** -0.5, 0.5, ((0, 4), (2, 8)))
    out_weight = bell_draw(keys[5], (SECTIONS, D, D), D ** -0.5, 0.0625, ((0, 4), (1, 8), (2, 8)))
    return {"section_input": section_input, "norm_gain": norm_gain, "in_weight": in_weight, "qkv_filters": qkv_filters, "mix_filter": mix_filter, "out_weight": out_weight}


NORM_EPS = 1e-05

def causal_mix(signal, tap_weights):
    tap_count = tap_weights.shape[0]
    length = signal.shape[0]
    padded = jnp.concatenate([jnp.zeros((tap_count - 1, signal.shape[1]), signal.dtype), signal], 0)

    def add_tap(index_tap, running):
        window = lax.dynamic_slice_in_dim(padded, tap_count - 1 - index_tap, length, 0)
        return running + tap_weights[index_tap] * window
    return lax.fori_loop(0, tap_count, add_tap, jnp.zeros(signal.shape, signal.dtype))

def reference(section_input, norm_gain, in_weight, qkv_filters, mix_filter, out_weight):
    results = []
    block_width = D // N_CTX
    for section in range(SECTIONS):
        incoming = section_input[section].astype(jnp.float32)
        squares = lax.optimization_barrier(jnp.sum(incoming * incoming, axis=1, keepdims=True))
        normed = (incoming * lax.rsqrt(squares / D + NORM_EPS) * norm_gain[section].astype(jnp.float32)).astype(jnp.bfloat16)
        weight_all = in_weight[section].reshape(D, 3 * D)
        summed_proj = jnp.zeros((SEGMENT, 3 * D), jnp.float32)
        for block in range(N_CTX):
            lower = block * block_width
            part_prod = jnp.dot(normed[:, lower:lower + block_width], weight_all[lower:lower + block_width], preferred_element_type=jnp.float32)
            summed_proj = summed_proj + part_prod.astype(jnp.bfloat16).astype(jnp.float32)
        projected = summed_proj.astype(jnp.bfloat16)
        filter_table = jnp.transpose(qkv_filters[section].astype(jnp.float32), (1, 0, 2)).reshape(TAPS, 3 * D)
        filtered = causal_mix(projected.astype(jnp.float32), filter_table).reshape(SEGMENT, 3, D)
        product = (filtered[:, 1] * filtered[:, 2]).astype(jnp.bfloat16)
        mixed = causal_mix(product.astype(jnp.float32), mix_filter[section].astype(jnp.float32))
        gated = (filtered[:, 0] * mixed).astype(jnp.bfloat16)
        block_out = (incoming + jnp.dot(gated, out_weight[section], preferred_element_type=jnp.float32)).astype(jnp.bfloat16)
        results.append(block_out)
    stacked = jnp.stack(results)
    return jnp.roll(stacked, 1, axis=0)
```

```python
import numpy as np
import jax
import jax.numpy as jnp
from jax import lax
from jax.experimental import pallas as pl
from jax.experimental.pallas import tpu as pltpu
from jax.sharding import PartitionSpec as P

D = 8192
NORM_EPS = 1e-05
BF = jnp.bfloat16
F32 = jnp.float32
B = 128
IN_CHUNKS = ((0,), (-1, 1), (-2, 2), (-3, 3, 4))
OUT_CHUNKS = ((-4, 3, -3, 2), (-2, 1, -1, 0))


def z_hop(value, steps):
    return lax.ppermute(value, "tp", [(s, (s + steps) % 8) for s in range(8)])


def x_hop(value, steps):
    return lax.ppermute(value, "ctx", [(s, s // 4 * 4 + (s % 4 + steps) % 4) for s in range(8)])


def swap(value, bit):
    return lax.ppermute(value, "ctx", [(s, s ^ bit) for s in range(8)])


def pipe_hop(value):
    return lax.ppermute(value, "pipe", [(s, (s + 1) % 4) for s in range(4)])


def split_bf16(values):
    high = values.astype(BF)
    low = (values - high.astype(np.float64)).astype(BF)
    return high, low


def dft_tables():
    k = np.arange(B)[:, None]
    n = np.arange(B)[None, :]
    angle = 2 * np.pi * ((k * n) % (2 * B)) / (2 * B)
    real, imag = np.cos(angle), -np.sin(angle)
    imag[0] = (-1.0) ** np.arange(B)
    forward = np.concatenate([real, imag], 0)
    weight = np.where(k == 0, 1.0, 2.0) / (2 * B)
    inv_real = (weight * np.cos(angle)).T
    inv_imag = (weight * -np.sin(angle)).T
    inv_imag[:, 0] = (-1.0) ** np.arange(B) / (2 * B)
    inverse = np.concatenate([inv_real, inv_imag], 1)
    return np.concatenate(split_bf16(forward), 0), np.concatenate(split_bf16(inverse), 0)


def project_kernel(n_rows, place, *refs):
    n = len(n_rows)
    pieces, (gain, weight), outs, sq, rows, acc = refs[:n], refs[n : n + 2], refs[n + 2 : n + 10], refs[n + 10], refs[-2], refs[-1]
    j = pl.program_id(0)

    @pl.when(j == 0)
    def _():
        at = 0
        sums = []
        for ref, count in zip(pieces, n_rows):
            v = ref[...].astype(F32)
            rows[at : at + count, :] = (v * gain[...].astype(F32)).astype(BF)
            v = v * v
            t = v[:, :B]
            for g in range(1, v.shape[1] // B):
                t = t + v[:, g * B : (g + 1) * B]
            sums.append(t)
            at += count
        t = jnp.concatenate(sums, 0)
        for i in range(at // B):
            sq[i : i + 1, :] = jnp.sum(t[i * B : (i + 1) * B].T, axis=0, keepdims=True)

    acc[...] = jnp.dot(rows[...], weight[0], preferred_element_type=F32).astype(BF)
    x, y = place[0] % 4, place[0] // 4
    col = pl.multiple_of(j * B, B)
    for i in range(8):
        dest = (x + 3 - i) % 4 + 4 * y if i < 4 else (x + i - 3) % 4 + 4 * (1 - y)
        outs[i][:, pl.ds(col, B)] = acc[:, pl.ds(pl.multiple_of(dest * B, B), B)]


def project(place, pieces, gain, weight):
    n_rows = tuple(p.shape[0] for p in pieces)
    total = sum(n_rows)
    whole = lambda shape: pl.BlockSpec(shape, lambda j, place: (0,) * len(shape))
    res = pl.pallas_call(
        lambda *refs: project_kernel(n_rows, *refs),
        grid_spec=pltpu.PrefetchScalarGridSpec(
            num_scalar_prefetch=1,
            grid=(3,),
            in_specs=[whole(p.shape) for p in pieces]
            + [whole(gain.shape), pl.BlockSpec((1, 1024, 1024), lambda j, place: (j, 0, 0))],
            out_specs=[whole((total, 3 * B))] * 8 + [whole((total // B, B))],
            scratch_shapes=[pltpu.VMEM((total, 1024), BF), pltpu.VMEM((total, 1024), BF)],
        ),
        out_shape=[jax.ShapeDtypeStruct((total, 3 * B), BF)] * 8 + [jax.ShapeDtypeStruct((total // B, B), F32)],
        compiler_params=pltpu.CompilerParams(vmem_limit_bytes=24 << 20),
        name="project",
    )(place, *pieces, gain, weight)
    return res[:8], res[8]


def filter_kernel(place, *refs):
    n = len(IN_CHUNKS)
    chunks, (sq, fq, fm, fwd, inv), outs = refs[:n], refs[n : n + 5], refs[n + 5 : n + 5 + len(OUT_CHUNKS)]
    proj, gate = refs[-2], refs[-1]
    tp = place[1]
    scale = lax.rsqrt(sq[...] / D + NORM_EPS)
    row = 0
    for ref, rels in zip(chunks, IN_CHUNKS):
        for i, rel in enumerate(rels):
            s = jnp.broadcast_to(scale[row : row + 1], (B, B)).T
            s = jnp.concatenate([s, s, s], 1)
            proj[(tp + rel + 8) % 8] = (ref[i * B : (i + 1) * B, :].astype(F32) * s).astype(BF)
            row += 1

    def spectrum(v):
        both = jnp.dot(fwd[...], v, preferred_element_type=F32)
        return both[:B] + both[2 * B : 3 * B], both[B : 2 * B] + both[3 * B :]

    def inverse(re, im):
        z = jnp.concatenate([re, im], 0)
        high = z.astype(BF)
        low = (z - high.astype(F32)).astype(BF)
        a = jnp.dot(inv[...], high, preferred_element_type=F32)
        return a[:B] + a[B:] + jnp.dot(inv[:B, :], low, preferred_element_type=F32)

    def filters(taps):
        re, im = spectrum(taps)
        first = lax.broadcasted_iota(jnp.int32, re.shape, 0) == 0
        return re, jnp.where(first, 0.0, im), jnp.where(first, im, re)

    def times(v, h):
        re, im = spectrum(v)
        return re * h[0] - im * h[1], re * h[1] + im * h[2]

    hq = filters(jnp.concatenate([fq[0, 0], fq[0, 1], fq[0, 2]], 1))
    hm = filters(fm[0])
    sign3 = jnp.where(lax.broadcasted_iota(jnp.int32, (B, 3 * B), 0) % 2 == 0, 1.0, -1.0)
    first3 = lax.broadcasted_iota(jnp.int32, (B, 3 * B), 0) == 0
    sign, first = sign3[:, :B], first3[:, :B]

    last, last_m = None, None
    for r in range(8):
        y = times(proj[r], hq)
        z = y if last is None else (y[0] + sign3 * last[0], y[1] + sign3 * last[1])
        last = y
        f = inverse(*z)
        product = (f[:, B : 2 * B] * f[:, 2 * B :]).astype(BF)
        y = times(product, hm)
        z = y if last_m is None else (y[0] + sign * last_m[0], y[1] + sign * last_m[1])
        last_m = y
        gate[r] = (f[:, :B] * inverse(*z)).astype(BF)
    for ref, rels in zip(outs, OUT_CHUNKS):
        for i, rel in enumerate(rels):
            ref[i * B : (i + 1) * B, :] = gate[(tp + rel + 8) % 8]


def filter_stage(place, chunks, squares, qkv_filters, mix_filter):
    fwd, inv = dft_tables()
    whole = lambda shape: pl.BlockSpec(shape, lambda i, place: (0,) * len(shape))
    return pl.pallas_call(
        filter_kernel,
        grid_spec=pltpu.PrefetchScalarGridSpec(
            num_scalar_prefetch=1,
            grid=(1,),
            in_specs=[whole(c.shape) for c in chunks]
            + [
                whole(squares.shape),
                pl.BlockSpec((1, 3, B, B), lambda i, place: (0, 0, 0, place[0])),
                pl.BlockSpec((1, B, B), lambda i, place: (0, 0, place[0])),
                whole(fwd.shape),
                whole(inv.shape),
            ],
            out_specs=[whole((len(r) * B, B)) for r in OUT_CHUNKS],
            scratch_shapes=[pltpu.VMEM((8, B, 3 * B), BF), pltpu.VMEM((8, B, B), BF)],
        ),
        out_shape=[jax.ShapeDtypeStruct((len(r) * B, B), BF) for r in OUT_CHUNKS],
        compiler_params=pltpu.CompilerParams(vmem_limit_bytes=24 << 20),
        name="filters",
    )(place, *chunks, squares, qkv_filters, mix_filter, jnp.asarray(fwd), jnp.asarray(inv))


def output_kernel(place, pair, up, down, far_up, far_down, weight, *refs):
    outs, rows = refs[:-1], refs[-1]
    x, y = place[0] % 4, place[0] // 4

    def put(value, dx, other):
        channel = (x + dx) % 4 + 4 * (1 - y if other else y)
        rows[:, pl.ds(pl.multiple_of(channel * B, B), B)] = value

    for o in range(2):
        put(pair[o], 0, o)
        put(up[o], 3, o)
        put(down[o], 1, o)
    put(far_up[...], 2, 0)
    put(far_down[...], 2, 1)
    for i, ref in enumerate(outs):
        ref[...] = jnp.dot(rows[i * B : (i + 1) * B, :], weight[...], preferred_element_type=F32).astype(BF)


def output_part(place, gathered, weight, n_blocks):
    whole = lambda shape: pl.BlockSpec(shape, lambda i, place: (0,) * len(shape))
    return pl.pallas_call(
        output_kernel,
        grid_spec=pltpu.PrefetchScalarGridSpec(
            num_scalar_prefetch=1,
            grid=(1,),
            in_specs=[whole(g.shape) for g in gathered] + [whole(weight.shape)],
            out_specs=[whole((B, 1024))] * n_blocks,
            scratch_shapes=[pltpu.VMEM((n_blocks * B, 1024), BF)],
        ),
        out_shape=[jax.ShapeDtypeStruct((B, 1024), BF)] * n_blocks,
        compiler_params=pltpu.CompilerParams(vmem_limit_bytes=24 << 20),
        name="output",
    )(place, *gathered, weight)


def on_device(section_input, norm_gain, in_weight, qkv_filters, mix_filter, out_weight):
    x = section_input[0]
    place = jnp.stack([lax.axis_index("ctx"), lax.axis_index("tp")]).astype(jnp.int32)
    weight_in = jnp.transpose(in_weight[0], (1, 0, 2))

    got = {0: (x,)}
    up = down = x
    for s in range(1, 4):
        up, down = z_hop(up, 1), z_hop(down, -1)
        got[-s], got[s] = (up,), (down,)
    got[4] = (z_hop(up[:64], 1), z_hop(down[64:], -1))

    chunks, sums = [], []
    for rels in IN_CHUNKS:
        parts, sq = project(place, [p for r in rels for p in got[r]], norm_gain, weight_in)
        up, down = parts[0], parts[4]
        for s in range(1, 4):
            up = x_hop(up, 1) + parts[s]
            down = x_hop(down, -1) + parts[4 + s]
        chunks.append(up + swap(down, 4))
        sums.append(sq)
    squares = jnp.concatenate(sums, 0)
    for bit in (4, 1, 2):
        squares = squares + swap(squares, bit)

    gated = filter_stage(place, chunks, squares, qkv_filters, mix_filter)

    blocks = {}
    for rels, mine in zip(OUT_CHUNKS, gated):
        pair = jnp.stack([mine, swap(mine, 4)])
        up, down = x_hop(pair, 1), x_hop(pair, -1)
        far_up, far_down = x_hop(up[0], 1), x_hop(down[1], -1)
        outs = output_part(place, (pair, up, down, far_up, far_down), out_weight[0], len(rels))
        blocks.update(zip(rels, outs))
    minus = blocks[-4]
    plus = blocks[3]
    for s in range(3, 0, -1):
        minus = z_hop(minus, -1) + blocks[-s]
        plus = z_hop(plus, 1)
        if s > 1:
            plus = plus + blocks[s - 1]
    minus = z_hop(minus, -1)
    total = blocks[0].astype(F32) + minus.astype(F32) + plus.astype(F32)
    return pipe_hop((x.astype(F32) + total).astype(BF))[None]


def solution(mesh):
    return jax.shard_map(
        on_device,
        mesh=mesh,
        in_specs=(
            P("pipe", "tp", "ctx"),
            P("pipe", "ctx"),
            P("pipe", "ctx", None, "tp"),
            P("pipe", None, None, "tp"),
            P("pipe", None, "tp"),
            P("pipe", "tp", "ctx"),
        ),
        out_specs=P("pipe", "tp", "ctx"),
        check_vma=False,
    )
```
